1024 devices in a mesh: section: 8 (over y, core), dp: 8 (over z_hi, x), mp: 16 (over z_lo).
Axes of the slice: x: 4, y: 4, z: 32 (z_hi: 2, z_lo: 16; z = z_hi * 16 + z_lo), core: 2. Of those that a mesh axis runs over, the one named last changes fastest.
Arguments:
- queries: bfloat16 [8, 3072, 4096], P('section', 'dp', 'mp'), may hold values from -200 to 200, as said below
- latents: bfloat16 [8, 512, 1280], P('dp', ('section', 'mp')), may hold values from -6 to 6
- key_weight: bfloat16 [8, 1280, 4096], P('section', None, 'mp'), may hold values from -0.15625 to 0.15625
- value_weight: bfloat16 [8, 1280, 4096], P('section', None, 'mp'), may hold values from -0.15625 to 0.15625
- out_weight: bfloat16 [8, 4096, 8192], P('section', 'mp'), may hold values from -0.375 to 0.375
- residual: bfloat16 [8, 3072, 8192], P('section', ('dp', 'mp')), may hold values from -3 to 3
- gate_angle: float32 [8], P('section'), may hold values from 0.3 to 1.2
- block_mask: int32 [8, 6, 8], P('dp'), may hold values from 0 to 1, as said below
Outputs:
- updated: bfloat16 [8, 3072, 8192], P('section', ('dp', 'mp'))
The draws below stay inside these ranges and needn't reach their ends.
Inputs may be any that keep to these rules, and one draw needn't show every extreme that they name: `block_mask`: entries are 0 or 1; some whole blocks see no image. `queries`: rows may differ in scale from one another by a factor of up to 100.
All inputs are finite; a program needn't handle non-finite values.
Results may differ from the reference program's by a relative error of at most 0.019.
Values may be sent and summed in bfloat16 or wider, within the bound.
A program may use at most 32 MiB of HBM per device.

```python
import jax
import jax.numpy as jnp
from jax import lax

D = 8192
VD = 1280
HEADS = 32
HEAD_DIM = 128
LEN = 384
IMG_DP = 8
ROWS = 512
HD = 4096
TOKENS = 3072
N_SECTION = 8
N_DP = 8
N_MP = 16


def draw_queries(key, part):
    full_shape = (N_SECTION, TOKENS, HEADS * HEAD_DIM)
    drawn = jax.random.normal(key, full_shape, jnp.float32)
    return jnp.clip(drawn, -200.0, 200.0).astype(jnp.bfloat16)


def draw_block_mask(key, part):
    full_shape = (N_DP, LEN // 64, IMG_DP)
    chosen = jax.random.randint(key, full_shape, 0, 2)
    block_kept = jax.random.randint(jax.random.fold_in(key, 3), (N_DP, LEN // 64, 1), 0, 4) > 0
    return jnp.where(block_kept, chosen, 0).astype(jnp.int32)


def steps_of(own_key, dims, cuts, smallest, top_value):
    factor_of = 1.0
    for position, parts in cuts:
        heights = jax.random.uniform(jax.random.fold_in(jax.random.fold_in(own_key, 6), position), (parts,), jnp.float32, smallest / len(cuts), top_value / len(cuts))
        factor_of = factor_of * jnp.repeat(jnp.exp(heights), dims[position] // parts).reshape((-1,) + (1,) * (len(dims) - 1 - position))
    return factor_of


def centred(rng, shape, scale, bound, split=(), held_as=jnp.bfloat16):
    entries = scale * jax.random.normal(rng, shape, jnp.float32)
    if split:
        entries = entries * steps_of(rng, shape, split, -0.22, 0.18)
    return jnp.clip(entries, -bound, bound).astype(held_as)


def setup_inputs(seed: int = 0) -> dict:
    keys = jax.random.split(jax.random.key(seed), 9)
    return {
        "queries": draw_queries(jax.random.fold_in(keys[8], 71), 0),
        "latents": centred(keys[1], (N_DP, ROWS, VD), 1.0, 6.0, ((0, 8), (1, 128))),
        "key_weight": centred(keys[2], (N_SECTION, VD, HD), VD ** -0.5, 0.15625, ((0, 8), (2, 16))),
        "value_weight": centred(keys[3], (N_SECTION, VD, HD), VD ** -0.5, 0.15625, ((0, 8), (2, 16))),
        "out_weight": centred(keys[4], (N_SECTION, HD, D), (HD // 16) ** -0.5, 0.375, ((0, 8), (1, 16))),
        "residual": centred(keys[5], (N_SECTION, TOKENS, D), 0.5, 3.0, ((0, 8), (1, 128))),
        "gate_angle": jnp.clip(0.3 + 0.90000004 * jax.random.uniform(keys[6], (N_SECTION,), jnp.float32) ** steps_of(keys[6], (N_SECTION,), ((0, 8),), -0.2, 0.2), 0.3, 1.2),
        "block_mask": draw_block_mask(jax.random.fold_in(keys[8], 71), 0),
    }


def token_mask(mask_table):
    blocks, images = mask_table.shape
    spread = jnp.broadcast_to(mask_table[:, None, :, None], (blocks, 64, images, 64))
    return spread.reshape(blocks * 64, images * 64) > 0


def attend(query_rows, key_rows, value_rows, mask_table):
    length = query_rows.shape[0]
    key_count = key_rows.shape[0]
    heads_here = query_rows.shape[1] // HEAD_DIM
    query_heads = query_rows.reshape(length, heads_here, HEAD_DIM).astype(jnp.float32)
    key_heads = key_rows.reshape(key_count, heads_here, HEAD_DIM).astype(jnp.float32)
    value_heads = value_rows.reshape(key_count, heads_here, HEAD_DIM).astype(jnp.float32)
    scores = jnp.einsum("thd,khd->htk", query_heads, key_heads) * (HEAD_DIM ** -0.5)
    allowed = token_mask(mask_table)[None]
    masked = jnp.where(allowed, scores, -1e30)
    row_max = jnp.max(masked, axis=-1, keepdims=True)
    any_live = jnp.any(allowed, axis=-1, keepdims=True)
    row_max = jnp.where(any_live, row_max, 0.0)
    numerators = jnp.exp(masked - row_max)
    denominator = jnp.maximum(jnp.sum(numerators, axis=-1, keepdims=True), 1.0)
    weights = (numerators / denominator).astype(jnp.bfloat16)
    attended = jnp.einsum("htk,khd->thd", weights.astype(jnp.float32), value_heads)
    return attended.reshape(length, heads_here * HEAD_DIM).astype(jnp.bfloat16)


def one_group(query_rows, latent_rows, key_proj, value_proj, out_proj, resid_rows, gate_value, mask_table):
    key_rows = jnp.dot(latent_rows, key_proj, preferred_element_type=jnp.float32).astype(jnp.bfloat16)
    value_rows = jnp.dot(latent_rows, value_proj, preferred_element_type=jnp.float32).astype(jnp.bfloat16)
    attended = attend(query_rows, key_rows, value_rows, mask_table)
    group_width = attended.shape[1] // N_MP

    def add_group(summed, group_idx):
        offset = group_idx * group_width
        column_part = lax.dynamic_slice_in_dim(attended, offset, group_width, 1)
        weight_part = lax.dynamic_slice_in_dim(out_proj, offset, group_width, 0)
        partial_value = jnp.dot(column_part, weight_part, preferred_element_type=jnp.float32).astype(jnp.bfloat16)
        partial_value = lax.optimization_barrier(partial_value)
        return summed + partial_value.astype(jnp.float32), None

    start_sum = jnp.zeros((attended.shape[0], out_proj.shape[1]), jnp.float32)
    summed, _ = lax.scan(add_group, start_sum, jnp.arange(N_MP, dtype=jnp.int32))
    return (resid_rows.astype(jnp.float32) + jnp.tanh(gate_value) * summed).astype(jnp.bfloat16)


def reference(queries, latents, key_weight, value_weight, out_weight, residual, gate_angle, block_mask):
    def per_section(section_idx):
        section_q = queries[section_idx].reshape(N_DP, LEN, queries.shape[2])
        section_r = residual[section_idx].reshape(N_DP, LEN, residual.shape[2])

        def per_group(dp_idx):
            return one_group(section_q[dp_idx], latents[dp_idx], key_weight[section_idx], value_weight[section_idx],
                             out_weight[section_idx], section_r[dp_idx], gate_angle[section_idx], block_mask[dp_idx])

        return lax.map(per_group, jnp.arange(N_DP, dtype=jnp.int32))

    result = lax.map(per_section, jnp.arange(N_SECTION, dtype=jnp.int32))
    return result.reshape(N_SECTION, N_DP * LEN, residual.shape[2])
```

```python
import functools

import jax
import jax.numpy as jnp
from jax import lax
from jax.experimental import pallas as pl
from jax.experimental.pallas import tpu as pltpu
from jax.sharding import PartitionSpec as P

HEAD_DIM = 128
CHUNKS = 4
TILE = 512
MESH = pl.DeviceIdType.MESH


def joined_along(blocks, dim):
    blocks = jnp.moveaxis(blocks, 0, dim)
    lengths = blocks.shape
    return blocks.reshape(*lengths[:dim], lengths[dim] * lengths[dim + 1], *lengths[dim + 2 :])


def from_everyone(x, axis):
    count = lax.axis_size(axis)
    return lax.all_to_all(jnp.broadcast_to(x[None], (count, *x.shape)), axis, 0, 0, tiled=True)


def gather_directly(x, axis, dim):
    return joined_along(from_everyone(x, axis), dim)


def token_mask(mask_table):
    blocks, images = mask_table.shape
    spread = jnp.broadcast_to(mask_table[:, None, :, None], (blocks, 64, images, 64))
    return spread.reshape(blocks * 64, images * 64) > 0


def attend(query_rows, key_rows, value_rows, allowed_rows):
    length = query_rows.shape[0]
    key_count = key_rows.shape[0]
    heads_here = query_rows.shape[1] // HEAD_DIM
    query_heads = query_rows.reshape(length, heads_here, HEAD_DIM)
    key_heads = key_rows.reshape(key_count, heads_here, HEAD_DIM)
    value_heads = value_rows.reshape(key_count, heads_here, HEAD_DIM)
    scores = jnp.einsum(
        "thd,khd->htk", query_heads, key_heads, preferred_element_type=jnp.float32
    ) * HEAD_DIM ** (-0.5)
    allowed = allowed_rows[None]
    masked = jnp.where(allowed, scores, -1e30)
    row_max = jnp.max(masked, axis=-1, keepdims=True)
    any_live = jnp.any(allowed, axis=-1, keepdims=True)
    row_max = jnp.where(any_live, row_max, 0.0)
    numerators = jnp.exp(masked - row_max)
    denominator = jnp.maximum(jnp.sum(numerators, axis=-1, keepdims=True), 1.0)
    weights = (numerators / denominator).astype(jnp.bfloat16)
    attended = jnp.einsum("htk,khd->thd", weights, value_heads, preferred_element_type=jnp.float32)
    return attended.reshape(length, heads_here * HEAD_DIM).astype(jnp.bfloat16)


def ring_place(n_mp):
    columns = lax.axis_size("dp") // 2
    half = lax.axis_index("dp") // columns
    column = lax.axis_index("dp") % columns
    return half * n_mp + lax.axis_index("mp"), column, columns


def ring_device(place, n_mp, column, columns):
    place = place % (2 * n_mp)
    return {"dp": (place // n_mp) * columns + column, "mp": place % n_mp}


def sum_kernel(
    n_mp, att_ref, w_ref, res_ref, gate_ref, out_ref,
    part, from_left, from_right, right_send, left_send, right_recv, left_recv,
):
    place, column, columns = ring_place(n_mp)
    me = lax.axis_index("mp")
    right = ring_device(place + 1, n_mp, column, columns)
    left = ring_device(place + 2 * n_mp - 1, n_mp, column, columns)
    far = n_mp // 2
    rows = out_ref.shape[0]
    width = w_ref.shape[1] // CHUNKS

    barrier = pltpu.get_barrier_semaphore()
    pl.semaphore_signal(barrier, inc=1, device_id=left, device_id_type=MESH)
    pl.semaphore_signal(barrier, inc=1, device_id=right, device_id_type=MESH)

    def to_right(step, c):
        block = (me + far - step + n_mp) % n_mp
        return pltpu.make_async_remote_copy(
            src_ref=part.at[c, block], dst_ref=from_left.at[step, c],
            send_sem=right_send.at[step, c], recv_sem=right_recv.at[step, c],
            device_id=right, device_id_type=MESH,
        )

    def to_left(step, c):
        block = (me - far + 1 + step + n_mp) % n_mp
        return pltpu.make_async_remote_copy(
            src_ref=part.at[c, block], dst_ref=from_right.at[step, c],
            send_sem=left_send.at[step, c], recv_sem=left_recv.at[step, c],
            device_id=left, device_id_type=MESH,
        )

    for c in range(CHUNKS):
        @pl.loop(0, width // TILE)
        def _(tile):
            columns_in = pl.ds(pl.multiple_of(c * width + tile * TILE, TILE), TILE)
            columns_out = pl.ds(pl.multiple_of(tile * TILE, TILE), TILE)
            term = jnp.dot(att_ref[...], w_ref[:, columns_in], preferred_element_type=jnp.float32)
            part[c, :, :, columns_out] = term.reshape(n_mp, rows, TILE).astype(jnp.bfloat16)

        if c == 0:
            pl.semaphore_wait(barrier, 2)
        to_right(0, c).start()
        to_left(0, c).start()

    def add_right(step, c):
        to_right(step - 1, c).wait_recv()
        block = (me + far - step + n_mp) % n_mp
        part[c, block] = (
            part[c, block].astype(jnp.float32) + from_left[step - 1, c].astype(jnp.float32)
        ).astype(jnp.bfloat16)
        to_right(step, c).start()

    def add_left(step, c):
        to_left(step - 1, c).wait_recv()
        block = (me - far + 1 + step + n_mp) % n_mp
        part[c, block] = (
            part[c, block].astype(jnp.float32) + from_right[step - 1, c].astype(jnp.float32)
        ).astype(jnp.bfloat16)
        to_left(step, c).start()

    @pl.loop(1, far - 1)
    def _(step):
        for c in range(CHUNKS):
            add_right(step, c)
            add_left(step, c)

    gate = jnp.tanh(gate_ref[...])
    for c in range(CHUNKS):
        add_right(far - 1, c)
    for c in range(CHUNKS):
        to_left(far - 2, c).wait_recv()
        to_right(far - 1, c).wait_recv()
        here = pl.ds(c * width, width)
        branch = (
            part[c, me].astype(jnp.float32)
            + from_left[far - 1, c].astype(jnp.float32)
            + from_right[far - 2, c].astype(jnp.float32)
        )
        out_ref[:, here] = (res_ref[:, here].astype(jnp.float32) + gate * branch).astype(jnp.bfloat16)

    @pl.loop(0, far - 1)
    def _(step):
        for c in range(CHUNKS):
            to_right(step, c).wait_send()
            to_left(step, c).wait_send()

    for c in range(CHUNKS):
        to_right(far - 1, c).wait_send()


def summed_branch(attended, out_proj, residual, gate):
    n_mp = lax.axis_size("mp")
    rows, wide = residual.shape
    far = n_mp // 2
    width = wide // CHUNKS
    return pl.pallas_call(
        functools.partial(sum_kernel, n_mp),
        out_shape=jax.ShapeDtypeStruct((rows, wide), jnp.bfloat16),
        in_specs=[pl.BlockSpec(memory_space=pltpu.VMEM)] * 4,
        out_specs=pl.BlockSpec(memory_space=pltpu.VMEM),
        scratch_shapes=[
            pltpu.VMEM((CHUNKS, n_mp, rows, width), jnp.bfloat16),
            pltpu.VMEM((far, CHUNKS, rows, width), jnp.bfloat16),
            pltpu.VMEM((far - 1, CHUNKS, rows, width), jnp.bfloat16),
            pltpu.SemaphoreType.DMA((far, CHUNKS)),
            pltpu.SemaphoreType.DMA((far - 1, CHUNKS)),
            pltpu.SemaphoreType.DMA((far, CHUNKS)),
            pltpu.SemaphoreType.DMA((far - 1, CHUNKS)),
        ],
        compiler_params=pltpu.CompilerParams(
            collective_id=0, has_side_effects=True, vmem_limit_bytes=60 * 2**20
        ),
        name="ring_sum",
    )(attended, out_proj, residual, gate)


def window_rows(attended):
    n_mp = lax.axis_size("mp")
    n_dp = lax.axis_size("dp")
    me = lax.axis_index("mp")
    length = attended.shape[0]
    upper = lax.slice_in_dim(attended, length // 2, length, axis=0)
    lower = lax.slice_in_dim(attended, 0, length // 2, axis=0)
    sent = jnp.where(me < n_mp // 2, upper, lower)
    pairs = [(d, (d + n_dp // 2) % n_dp) for d in range(n_dp)]
    came = lax.ppermute(sent, "dp", pairs)
    other = jnp.concatenate([came, came], axis=0)
    offset = jnp.arange(length) // (length // n_mp) - me
    own = (offset > -(n_mp // 2)) & (offset <= n_mp // 2)
    return jnp.where(own[:, None], attended, other)


def local(queries, latents, key_weight, value_weight, out_weight, residual, gate_angle, block_mask):
    local_rows = gather_directly(latents, "mp", 1)
    flat_rows = gather_directly(local_rows, "section", 1)[0]
    key_rows = jnp.dot(flat_rows, key_weight[0], preferred_element_type=jnp.float32).astype(jnp.bfloat16)
    value_rows = jnp.dot(flat_rows, value_weight[0], preferred_element_type=jnp.float32).astype(jnp.bfloat16)
    attended = attend(queries[0], key_rows, value_rows, token_mask(block_mask[0]))
    gate = jnp.broadcast_to(gate_angle.reshape(1, 1), (1, 128))[:, :1]
    updated = summed_branch(window_rows(attended), out_weight[0], residual[0], gate)
    return updated[None]


def solution(mesh):
    return jax.shard_map(
        local,
        mesh=mesh,
        in_specs=(
            P("section", "dp", "mp"),
            P("dp", ("section", "mp"), None),
            P("section", None, "mp"),
            P("section", None, "mp"),
            P("section", "mp", None),
            P("section", ("dp", "mp"), None),
            P("section"),
            P("dp", None, None),
        ),
        out_specs=P("section", ("dp", "mp"), None),
        check_vma=False,
    )
```
